32 devices in a mesh: layer: 2 (over core), rows: 16 (over z, y, x).
Axes of the slice: x: 2, y: 2, z: 4, core: 2. Of those that a mesh axis runs over, the one named last changes fastest.
Arguments:
- frames: bfloat16 [3, 32, 256, 256], P(None, 'rows'), may hold values from -6 to 6
- initial_state: bfloat16 [2, 32, 256, 256], P('layer', 'rows'), may hold values from -3 to 3
- w_gates: bfloat16 [2, 3, 3, 512, 512], P('layer'), may hold values from -0.25 to 0.25
- w_cand: bfloat16 [2, 3, 3, 512, 256], P('layer'), may hold values from -0.125 to 0.125
- biases: float32 [2, 768], P('layer'), may hold values from -4 to 4
Outputs:
- hidden_frames: bfloat16 [2, 3, 32, 256, 256], P('layer', None, 'rows')
The draws below stay inside these ranges and needn't reach their ends.
All inputs are finite; a program needn't handle non-finite values.
Results may differ from the reference program's by a relative error of at most 0.0048.
Values may be sent and summed in bfloat16 or wider, within the bound.
A program may use at most 64 MiB of HBM per device.

```python
import jax
import jax.numpy as jnp

CH = 256
COLS = 256
FRAMES = 3
LAYERS = 2
GRID_ROWS = 32


def block_scale(key, dims, cuts, low, largest):
    def one(position, shards_of):
        draws = jax.random.uniform(jax.random.fold_in(jax.random.fold_in(key, 6), position), (shards_of,), jnp.float32, low / len(cuts), largest / len(cuts))
        return jnp.repeat(jnp.exp(draws), dims[position] // shards_of).reshape((-1,) + (1,) * (len(dims) - position - 1))

    factor_of = one(*cuts[0])
    for cut in cuts[1:]:
        factor_of = factor_of * one(*cut)
    return factor_of


def normal_values(rng, extent, width, limit, cuts=(), held_as=jnp.bfloat16):
    values = width * jax.random.normal(rng, extent, jnp.float32)
    if cuts:
        values = values * block_scale(rng, extent, cuts, -0.22, 0.18)
    return jnp.clip(values, -limit, limit).astype(held_as)


def setup_inputs(seed: int = 0) -> dict:
    arg_keys = jax.random.split(jax.random.key(seed), 6)
    return {
        "frames": normal_values(arg_keys[0], (FRAMES, GRID_ROWS, COLS, CH), 1.0, 6.0, ((1, 16),)),
        "initial_state": normal_values(arg_keys[1], (LAYERS, GRID_ROWS, COLS, CH), 1.2, 3.0, ((0, 2), (1, 16))),
        "w_gates": normal_values(arg_keys[2], (LAYERS, 3, 3, 2 * CH, 2 * CH), (5 * CH // 2) ** -0.5, 0.25, ((0, 2),)),
        "w_cand": normal_values(arg_keys[3], (LAYERS, 3, 3, 2 * CH, CH), (9 * CH) ** -0.5, 0.125, ((0, 2),)),
        "biases": normal_values(arg_keys[4], (LAYERS, 3 * CH), 1.0, 4.0, ((0, 2),), jnp.float32),
    }


def convolve(source_rows, weight):
    row_count, col_count, _ = source_rows.shape
    padded = jnp.pad(source_rows, ((1, 1), (1, 1), (0, 0)))
    summed = jnp.zeros((row_count * col_count, weight.shape[3]), jnp.float32)
    for row_off in range(3):
        for col_off in range(3):
            tap_view = padded[row_off:row_off + row_count, col_off:col_off + col_count].reshape(row_count * col_count, -1)
            summed = summed + jnp.dot(tap_view, weight[row_off, col_off], preferred_element_type=jnp.float32)
    return summed.reshape(row_count, col_count, -1)


def reference(frames, initial_state, w_gates, w_cand, biases):
    channels = initial_state.shape[-1]
    sequence = frames
    collected = []
    for layer_idx in range(LAYERS):
        hidden = initial_state[layer_idx]
        produced = []
        for frame_idx in range(FRAMES):
            inputs = sequence[frame_idx]
            gate_pre = convolve(jnp.concatenate([inputs, hidden], -1), w_gates[layer_idx]) + biases[layer_idx, :2 * channels]
            gate_all = jax.nn.sigmoid(gate_pre)
            update = gate_all[..., :channels]
            reset_gate = gate_all[..., channels:]
            reset_state = (reset_gate * hidden.astype(jnp.float32)).astype(jnp.bfloat16)
            candidate = jnp.tanh(convolve(jnp.concatenate([inputs, reset_state], -1), w_cand[layer_idx]) + biases[layer_idx, 2 * channels:])
            hidden = ((1.0 - update) * hidden.astype(jnp.float32) + update * candidate).astype(jnp.bfloat16)
            produced.append(hidden)
        sequence = jnp.stack(produced)
        collected.append(sequence)
    return jnp.stack(collected)
```

```python
import functools

import jax
import jax.numpy as jnp
from jax import lax
from jax.experimental import pallas as pl
from jax.experimental.pallas import tpu as pltpu
from jax.sharding import PartitionSpec as P

MESH = pltpu.DeviceIdType.MESH if hasattr(pltpu, "DeviceIdType") else pl.DeviceIdType.MESH

COL_DIRS = ((0, -1), (0, 1), (-1, -1), (-1, 1), (1, -1), (1, 1))


def reorder(c, group):
    if group == 4:
        return c + (c // 2) * (5 - 2 * c)
    return c


def kernel(
    count, group, frames_ref, init_ref, wg_ref, wc_ref, bias_ref, out_ref,
    wg, wc, xs, hs, rs, im, upd, part,
    row_halo, rs_row_halo, col_stage, col_halo, rs_col_stage, rs_col_halo,
    w_sem, own_sem, init_send, init_recv, x_send, x_recv, pass_send, pass_recv,
    out_own, out_send, out_recv,
    row_send, row_recv, col_send, col_recv,
    rrow_send, rrow_recv, rcol_send, rcol_recv,
):
    frame_count, strip, cols, ch = frames_ref.shape
    height = strip * group
    width = cols // group
    tile = height * width
    layer = lax.axis_index("layer")
    last_layer = lax.axis_size("layer") - 1
    index = lax.axis_index("rows")
    planes = count // group
    q = index // group
    c = index % group
    t = reorder(c, group)

    def at(plane, tile_index):
        return {"rows": plane * group + reorder(tile_index, group)}

    def guarded(step_row, step_col, action):
        terms = []
        if step_row < 0:
            terms.append(q > 0)
        if step_row > 0:
            terms.append(q < planes - 1)
        if step_col < 0:
            terms.append(t > 0)
        if step_col > 0:
            terms.append(t < group - 1)
        cond = functools.reduce(jnp.logical_and, terms)
        pl.when(cond)(action)

    copy_wg = pltpu.make_async_copy(wg_ref, wg, w_sem.at[0])
    copy_wc = pltpu.make_async_copy(wc_ref, wc, w_sem.at[1])
    own_cols = pl.ds(pl.multiple_of(t * width, width), width)
    own_rows = pl.ds(c * strip, strip)

    def own_init():
        return pltpu.make_async_copy(init_ref.at[:, own_cols, :], hs.at[0, own_rows], own_sem.at[0])

    def own_frame(f):
        return pltpu.make_async_copy(
            frames_ref.at[f, :, own_cols, :], xs.at[f, own_rows], own_sem.at[1]
        )

    def member(d):
        return lax.rem(c + d, group)

    def init_copy(d):
        target = member(d)
        tcols = pl.ds(pl.multiple_of(reorder(target, group) * width, width), width)
        return pltpu.make_async_remote_copy(
            src_ref=init_ref.at[:, tcols, :], dst_ref=hs.at[0, own_rows],
            send_sem=init_send.at[d], recv_sem=init_recv.at[d],
            device_id={"rows": q * group + target}, device_id_type=MESH,
        )

    def frame_copy(f, d):
        target = member(d)
        tcols = pl.ds(pl.multiple_of(reorder(target, group) * width, width), width)
        return pltpu.make_async_remote_copy(
            src_ref=frames_ref.at[f, :, tcols, :], dst_ref=xs.at[f, own_rows],
            send_sem=x_send.at[f, d], recv_sem=x_recv.at[f, d],
            device_id={"rows": q * group + target}, device_id_type=MESH,
        )

    def pass_copy(f):
        return pltpu.make_async_remote_copy(
            src_ref=hs.at[f + 1], dst_ref=xs.at[f],
            send_sem=pass_send.at[f], recv_sem=pass_recv.at[f],
            device_id={"layer": jnp.minimum(layer + 1, last_layer)}, device_id_type=MESH,
        )

    def out_copy(f, d):
        target = member(d)
        return pltpu.make_async_remote_copy(
            src_ref=hs.at[f + 1, pl.ds(target * strip, strip)],
            dst_ref=out_ref.at[0, f, :, own_cols, :],
            send_sem=out_send.at[f, d], recv_sem=out_recv.at[f, d],
            device_id={"rows": q * group + target}, device_id_type=MESH,
        )

    def own_out(f):
        return pltpu.make_async_copy(
            hs.at[f + 1, own_rows], out_ref.at[0, f, :, own_cols, :], out_own.at[f]
        )

    copy_wg.start()
    copy_wc.start()
    own_init().start()
    pl.when(layer == 0)(lambda: own_frame(0).start())

    row_halo[...] = jnp.zeros_like(row_halo)
    rs_row_halo[...] = jnp.zeros_like(rs_row_halo)
    col_halo[...] = jnp.zeros_like(col_halo)
    rs_col_halo[...] = jnp.zeros_like(rs_col_halo)

    barrier = pltpu.get_barrier_semaphore()

    def greet(where):
        pl.semaphore_signal(barrier, inc=1, device_id=where, device_id_type=MESH)

    for d in range(1, group):
        greet({"rows": q * group + member(d)})
    for step in (-1, 1):
        for side in (-1, 0, 1):
            guarded(step, side, lambda step=step, side=side: greet(at(q + step, t + side)))
    pl.when(layer > 0)(lambda: greet({"layer": layer - 1}))
    pl.when(layer < last_layer)(lambda: greet({"layer": layer + 1}))
    one = lambda cond: jnp.where(cond, 1, 0)
    sideways = 1 + one(t > 0) + one(t < group - 1)
    upright = one(q > 0) + one(q < planes - 1)
    pl.semaphore_wait(
        barrier, group - 1 + sideways * upright + one(layer > 0) + one(layer < last_layer)
    )

    for d in range(1, group):
        init_copy(d).start()

    @pl.when(layer == 0)
    def _():
        for d in range(1, group):
            frame_copy(0, d).start()

    own_init().wait()
    for d in range(1, group):
        init_copy(d).wait()

    def exchange(row_pairs, row_out, row_in, stage, halo, col_out, col_in, start):
        def run(copy):
            if start:
                copy.start()
            else:
                copy.wait()

        for side, step in enumerate((-1, 1)):
            for kind, (field, dest) in enumerate(row_pairs):
                def row(side=side, step=step, kind=kind, field=field, dest=dest):
                    run(pltpu.make_async_remote_copy(
                        src_ref=field.at[0 if step < 0 else height - 1],
                        dst_ref=dest.at[1 - side],
                        send_sem=row_out.at[kind, side], recv_sem=row_in.at[kind, 1 - side],
                        device_id=at(q + step, t), device_id_type=MESH,
                    ))

                if start:
                    guarded(step, 0, row)
                else:
                    def both(side=side, step=step, kind=kind, field=field, dest=dest):
                        copy = pltpu.make_async_remote_copy(
                            src_ref=field.at[0], dst_ref=dest.at[side],
                            send_sem=row_out.at[kind, side], recv_sem=row_in.at[kind, side],
                            device_id=at(q + step, t), device_id_type=MESH,
                        )
                        copy.wait()

                    guarded(step, 0, both)
        for k, (dr, dc) in enumerate(COL_DIRS):
            back = COL_DIRS.index((-dr, -dc))

            def col(k=k, back=back, dr=dr, dc=dc):
                copy = pltpu.make_async_remote_copy(
                    src_ref=stage.at[0 if dc < 0 else 1],
                    dst_ref=halo.at[back if start else k],
                    send_sem=col_out.at[k], recv_sem=col_in.at[back if start else k],
                    device_id=at(q + dr, t + dc), device_id_type=MESH,
                )
                run(copy)

            guarded(dr, dc, col)

    first_col = lax.broadcasted_iota(jnp.int32, (width, ch), 0) == 0
    last_col = lax.broadcasted_iota(jnp.int32, (width, ch), 0) == width - 1

    def spread(load, halo, lanes, base):
        for i in range(height + 2):
            v = load(i).astype(jnp.float32)
            if i == 0:
                left = halo[2, height - 1 : height, lanes]
                right = halo[3, height - 1 : height, lanes]
            elif i == height + 1:
                left, right = halo[4, 0:1, lanes], halo[5, 0:1, lanes]
            else:
                left, right = halo[0, i - 1 : i, lanes], halo[1, i - 1 : i, lanes]
            before = jnp.where(first_col, jnp.broadcast_to(left, v.shape), pltpu.roll(v, 1, 0))
            after = jnp.where(
                last_col, jnp.broadcast_to(right, v.shape), pltpu.roll(v, width - 1, 0)
            )
            rows = slice(i * width, (i + 1) * width)
            for b, piece in enumerate((before, v, after)):
                lo = b * 2 * ch + base
                im[rows, lo : lo + ch] = piece.astype(jnp.bfloat16)

    def lhs(a, lo, size):
        return im[a * width : a * width + tile, lo : lo + size]

    def full(weight, n_lo):
        total = None
        for a in range(3):
            term = jnp.dot(
                lhs(a, 0, 6 * ch), weight[a, :, n_lo : n_lo + ch],
                preferred_element_type=jnp.float32,
            )
            total = term if total is None else total + term
        return total

    def half(weight, base):
        total = None
        for a in range(3):
            for b in range(3):
                lo = b * 2 * ch + base
                term = jnp.dot(
                    lhs(a, lo, ch), weight[a, lo : lo + ch, :],
                    preferred_element_type=jnp.float32,
                )
                total = term if total is None else total + term
        return total

    def step(f, carry):
        @pl.when(layer == 0)
        def _():
            own_frame(f).wait()
            for d in range(1, group):
                frame_copy(f, d).wait()

        @pl.when(layer > 0)
        def _():
            pass_copy(f).wait_recv()

        for i in range(height):
            for k, field in enumerate((xs.at[f], hs.at[f])):
                v = field[i].astype(jnp.float32)
                lanes = slice(k * ch, (k + 1) * ch)
                col_stage[0, i : i + 1, lanes] = v[0:1]
                col_stage[1, i : i + 1, lanes] = v[width - 1 : width]
        args = (
            ((xs.at[f], row_halo.at[0]), (hs.at[f], row_halo.at[1])),
            row_send, row_recv, col_stage, col_halo, col_send, col_recv,
        )
        exchange(*args, True)
        exchange(*args, False)

        @pl.when(jnp.logical_and(layer == 0, f + 1 < frame_count))
        def _():
            own_frame(f + 1).start()
            for d in range(1, group):
                frame_copy(f + 1, d).start()

        for k, field in enumerate((xs, hs)):
            def load(i, k=k, field=field):
                if i == 0:
                    return row_halo[k, 0]
                if i == height + 1:
                    return row_halo[k, 1]
                return field[f, i - 1]

            spread(load, col_halo, slice(k * ch, (k + 1) * ch), k * ch)

        pl.when(f == 0)(lambda: copy_wg.wait())
        reset = jax.nn.sigmoid(full(wg, ch) + bias_ref[:, ch : 2 * ch])
        hidden = hs[f].reshape(tile, ch).astype(jnp.float32)
        rs[...] = (reset * hidden).astype(jnp.bfloat16).reshape(height, width, ch)
        for i in range(height):
            v = rs[i].astype(jnp.float32)
            rs_col_stage[0, i : i + 1, :] = v[0:1]
            rs_col_stage[1, i : i + 1, :] = v[width - 1 : width]
        args = (
            ((rs, rs_row_halo),),
            rrow_send, rrow_recv, rs_col_stage, rs_col_halo, rcol_send, rcol_recv,
        )
        exchange(*args, True)
        upd[...] = jax.nn.sigmoid(full(wg, 0) + bias_ref[:, 0:ch])
        pl.when(f == 0)(lambda: copy_wc.wait())
        part[...] = half(wc, 0) + bias_ref[:, 2 * ch : 3 * ch]
        exchange(*args, False)

        def load_reset(i):
            if i == 0:
                return rs_row_halo[0]
            if i == height + 1:
                return rs_row_halo[1]
            return rs[i - 1]

        spread(load_reset, rs_col_halo, slice(0, ch), ch)
        candidate = jnp.tanh(part[...] + half(wc, ch))
        update = upd[...]
        hidden = hs[f].reshape(tile, ch).astype(jnp.float32)
        fresh = (1.0 - update) * hidden + update * candidate
        hs[f + 1] = fresh.astype(jnp.bfloat16).reshape(height, width, ch)
        pl.when(layer < last_layer)(lambda: pass_copy(f).start())
        own_out(f).start()
        for d in range(1, group):
            out_copy(f, d).start()
        return carry

    lax.fori_loop(0, frame_count, step, 0)

    def finish(f, carry):
        pl.when(layer < last_layer)(lambda: pass_copy(f).wait_send())
        own_out(f).wait()
        for d in range(1, group):
            out_copy(f, d).wait()
        return carry

    lax.fori_loop(0, frame_count, finish, 0)


def shards(count, frames, initial_state, w_gates, w_cand, biases):
    frame_count, strip, cols, ch = frames.shape
    group = 4 if count % 4 == 0 else 1
    height, width = strip * group, cols // group
    dma = pltpu.SemaphoreType.DMA
    bf16, f32 = jnp.bfloat16, jnp.float32
    anywhere = pl.BlockSpec(memory_space=pl.ANY)
    rows_k = w_gates.shape[2] * w_gates.shape[3]
    tile = height * width
    return pl.pallas_call(
        functools.partial(kernel, count, group),
        out_shape=jax.ShapeDtypeStruct((1, frame_count, strip, cols, ch), bf16),
        in_specs=[anywhere] * 4 + [pl.BlockSpec(memory_space=pltpu.VMEM)],
        out_specs=anywhere,
        scratch_shapes=[
            pltpu.VMEM((3, rows_k, 2 * ch), bf16),
            pltpu.VMEM((3, rows_k, ch), bf16),
            pltpu.VMEM((frame_count, height, width, ch), bf16),
            pltpu.VMEM((frame_count + 1, height, width, ch), bf16),
            pltpu.VMEM((height, width, ch), bf16),
            pltpu.VMEM(((height + 2) * width, 6 * ch), bf16),
            pltpu.VMEM((tile, ch), f32),
            pltpu.VMEM((tile, ch), f32),
            pltpu.VMEM((2, 2, width, ch), bf16),
            pltpu.VMEM((2, width, ch), bf16),
            pltpu.VMEM((2, height, 2 * ch), f32),
            pltpu.VMEM((6, height, 2 * ch), f32),
            pltpu.VMEM((2, height, ch), f32),
            pltpu.VMEM((6, height, ch), f32),
            dma((2,)), dma((2,)), dma((group,)), dma((group,)),
            dma((frame_count, group)), dma((frame_count, group)),
            dma((frame_count,)), dma((frame_count,)),
            dma((frame_count,)), dma((frame_count, group)), dma((frame_count, group)),
            dma((2, 2)), dma((2, 2)), dma((6,)), dma((6,)),
            dma((1, 2)), dma((1, 2)), dma((6,)), dma((6,)),
        ],
        compiler_params=pltpu.CompilerParams(
            collective_id=0, has_side_effects=True, vmem_limit_bytes=48 * 1024 * 1024
        ),
    )(
        frames,
        initial_state[0],
        w_gates.reshape(3, rows_k, 2 * ch),
        w_cand.reshape(3, rows_k, ch),
        biases,
    )


def solution(mesh):
    placed = (
        P(None, "rows", None, None),
        P("layer", "rows", None, None),
        P("layer", None, None, None, None),
        P("layer", None, None, None, None),
        P("layer", None),
    )
    return jax.shard_map(
        functools.partial(shards, mesh.shape["rows"]),
        mesh=mesh,
        in_specs=placed,
        out_specs=P("layer", None, "rows", None, None),
        check_vma=False,
    )
```

```python
import functools

import jax
import jax.numpy as jnp
from jax import lax
from jax.experimental import pallas as pl
from jax.experimental.pallas import tpu as pltpu
from jax.sharding import PartitionSpec as P

MESH = pltpu.DeviceIdType.MESH if hasattr(pltpu, "DeviceIdType") else pl.DeviceIdType.MESH

COL_DIRS = ((0, -1), (0, 1), (-1, -1), (-1, 1), (1, -1), (1, 1))


def reorder(c, group):
    if group == 4:
        return c + (c // 2) * (5 - 2 * c)
    return c


def kernel(
    count, group, frames_ref, init_ref, wg_ref, wc_ref, bias_ref, out_ref,
    wg, wc, xs, hs, rs, im, upd, part,
    row_halo, rs_row_halo, col_stage, col_halo, rs_col_stage, rs_col_halo,
    w_sem, own_sem, init_send, init_recv, x_send, x_recv, pass_send, pass_recv,
    out_own, out_send, out_recv,
    row_send, row_recv, col_send, col_recv,
    rrow_send, rrow_recv, rcol_send, rcol_recv,
):
    frame_count, strip, cols, ch = frames_ref.shape
    height = strip * group
    width = cols // group
    tile = height * width
    layer = lax.axis_index("layer")
    last_layer = lax.axis_size("layer") - 1
    index = lax.axis_index("rows")
    planes = count // group
    q = index // group
    c = index % group
    t = reorder(c, group)

    def at(plane, tile_index):
        return {"rows": plane * group + reorder(tile_index, group)}

    def guarded(step_row, step_col, action):
        terms = []
        if step_row < 0:
            terms.append(q > 0)
        if step_row > 0:
            terms.append(q < planes - 1)
        if step_col < 0:
            terms.append(t > 0)
        if step_col > 0:
            terms.append(t < group - 1)
        cond = functools.reduce(jnp.logical_and, terms)
        pl.when(cond)(action)

    copy_wg = pltpu.make_async_copy(wg_ref, wg, w_sem.at[0])
    copy_wc = pltpu.make_async_copy(wc_ref, wc, w_sem.at[1])
    own_cols = pl.ds(pl.multiple_of(t * width, width), width)
    own_rows = pl.ds(c * strip, strip)

    def own_init():
        return pltpu.make_async_copy(init_ref.at[:, own_cols, :], hs.at[0, own_rows], own_sem.at[0])

    def own_frame(f):
        return pltpu.make_async_copy(
            frames_ref.at[f, :, own_cols, :], xs.at[f, own_rows], own_sem.at[1]
        )

    def member(d):
        return lax.rem(c + d, group)

    def init_copy(d):
        target = member(d)
        tcols = pl.ds(pl.multiple_of(reorder(target, group) * width, width), width)
        return pltpu.make_async_remote_copy(
            src_ref=init_ref.at[:, tcols, :], dst_ref=hs.at[0, own_rows],
            send_sem=init_send.at[d], recv_sem=init_recv.at[d],
            device_id={"rows": q * group + target}, device_id_type=MESH,
        )

    def frame_copy(f, d):
        target = member(d)
        tcols = pl.ds(pl.multiple_of(reorder(target, group) * width, width), width)
        return pltpu.make_async_remote_copy(
            src_ref=frames_ref.at[f, :, tcols, :], dst_ref=xs.at[f, own_rows],
            send_sem=x_send.at[f, d], recv_sem=x_recv.at[f, d],
            device_id={"rows": q * group + target}, device_id_type=MESH,
        )

    def pass_copy(f):
        return pltpu.make_async_remote_copy(
            src_ref=hs.at[f + 1], dst_ref=xs.at[f],
            send_sem=pass_send.at[f], recv_sem=pass_recv.at[f],
            device_id={"layer": jnp.minimum(layer + 1, last_layer)}, device_id_type=MESH,
        )

    def out_copy(f, d):
        target = member(d)
        return pltpu.make_async_remote_copy(
            src_ref=hs.at[f + 1, pl.ds(target * strip, strip)],
            dst_ref=out_ref.at[0, f, :, own_cols, :],
            send_sem=out_send.at[f, d], recv_sem=out_recv.at[f, d],
            device_id={"rows": q * group + target}, device_id_type=MESH,
        )

    def own_out(f):
        return pltpu.make_async_copy(
            hs.at[f + 1, own_rows], out_ref.at[0, f, :, own_cols, :], out_own.at[f]
        )

    copy_wg.start()
    copy_wc.start()
    own_init().start()
    pl.when(layer == 0)(lambda: own_frame(0).start())

    row_halo[...] = jnp.zeros_like(row_halo)
    rs_row_halo[...] = jnp.zeros_like(rs_row_halo)
    col_halo[...] = jnp.zeros_like(col_halo)
    rs_col_halo[...] = jnp.zeros_like(rs_col_halo)

    barrier = pltpu.get_barrier_semaphore()

    def greet(where):
        pl.semaphore_signal(barrier, inc=1, device_id=where, device_id_type=MESH)

    for d in range(1, group):
        greet({"rows": q * group + member(d)})
    for step in (-1, 1):
        for side in (-1, 0, 1):
            guarded(step, side, lambda step=step, side=side: greet(at(q + step, t + side)))
    pl.when(layer > 0)(lambda: greet({"layer": layer - 1}))
    pl.when(layer < last_layer)(lambda: greet({"layer": layer + 1}))
    one = lambda cond: jnp.where(cond, 1, 0)
    sideways = 1 + one(t > 0) + one(t < group - 1)
    upright = one(q > 0) + one(q < planes - 1)
    pl.semaphore_wait(
        barrier, group - 1 + sideways * upright + one(layer > 0) + one(layer < last_layer)
    )

    for d in range(1, group):
        init_copy(d).start()

    @pl.when(layer == 0)
    def _():
        for d in range(1, group):
            frame_copy(0, d).start()

    own_init().wait()
    for d in range(1, group):
        init_copy(d).wait()

    def exchange(row_pairs, row_out, row_in, stage, halo, col_out, col_in, start):
        def run(copy):
            if start:
                copy.start()
            else:
                copy.wait()

        for side, step in enumerate((-1, 1)):
            for kind, (field, dest) in enumerate(row_pairs):
                def row(side=side, step=step, kind=kind, field=field, dest=dest):
                    run(pltpu.make_async_remote_copy(
                        src_ref=field.at[0 if step < 0 else height - 1],
                        dst_ref=dest.at[1 - side],
                        send_sem=row_out.at[kind, side], recv_sem=row_in.at[kind, 1 - side],
                        device_id=at(q + step, t), device_id_type=MESH,
                    ))

                if start:
                    guarded(step, 0, row)
                else:
                    def both(side=side, step=step, kind=kind, field=field, dest=dest):
                        copy = pltpu.make_async_remote_copy(
                            src_ref=field.at[0], dst_ref=dest.at[side],
                            send_sem=row_out.at[kind, side], recv_sem=row_in.at[kind, side],
                            device_id=at(q + step, t), device_id_type=MESH,
                        )
                        copy.wait()

                    guarded(step, 0, both)
        for k, (dr, dc) in enumerate(COL_DIRS):
            back = COL_DIRS.index((-dr, -dc))

            def col(k=k, back=back, dr=dr, dc=dc):
                copy = pltpu.make_async_remote_copy(
                    src_ref=stage.at[0 if dc < 0 else 1],
                    dst_ref=halo.at[back if start else k],
                    send_sem=col_out.at[k], recv_sem=col_in.at[back if start else k],
                    device_id=at(q + dr, t + dc), device_id_type=MESH,
                )
                run(copy)

            guarded(dr, dc, col)

    first_col = lax.broadcasted_iota(jnp.int32, (width, ch), 0) == 0
    last_col = lax.broadcasted_iota(jnp.int32, (width, ch), 0) == width - 1

    def spread(load, halo, lanes, base):
        for i in range(height + 2):
            v = load(i).astype(jnp.float32)
            if i == 0:
                left = halo[2, height - 1 : height, lanes]
                right = halo[3, height - 1 : height, lanes]
            elif i == height + 1:
                left, right = halo[4, 0:1, lanes], halo[5, 0:1, lanes]
            else:
                left, right = halo[0, i - 1 : i, lanes], halo[1, i - 1 : i, lanes]
            before = jnp.where(first_col, jnp.broadcast_to(left, v.shape), pltpu.roll(v, 1, 0))
            after = jnp.where(
                last_col, jnp.broadcast_to(right, v.shape), pltpu.roll(v, width - 1, 0)
            )
            rows = slice(i * width, (i + 1) * width)
            for b, piece in enumerate((before, v, after)):
                lo = b * 2 * ch + base
                im[rows, lo : lo + ch] = piece.astype(jnp.bfloat16)

    def lhs(a, lo, size):
        return im[a * width : a * width + tile, lo : lo + size]

    def full(weight, n_lo):
        return jnp.dot(
            jnp.concatenate([lhs(a, 0, 6 * ch) for a in range(3)], axis=1),
            weight[:, :, n_lo : n_lo + ch].reshape(18 * ch, ch),
            preferred_element_type=jnp.float32,
        )

    def half(weight, base):
        places = [(a, b * 2 * ch + base) for a in range(3) for b in range(3)]
        return jnp.dot(
            jnp.concatenate([lhs(a, lo, ch) for a, lo in places], axis=1),
            jnp.concatenate([weight[a, lo : lo + ch, :] for a, lo in places], axis=0),
            preferred_element_type=jnp.float32,
        )

    def step(f, carry):
        @pl.when(layer == 0)
        def _():
            own_frame(f).wait()
            for d in range(1, group):
                frame_copy(f, d).wait()

        @pl.when(layer > 0)
        def _():
            pass_copy(f).wait_recv()

        for i in range(height):
            for k, field in enumerate((xs.at[f], hs.at[f])):
                v = field[i].astype(jnp.float32)
                lanes = slice(k * ch, (k + 1) * ch)
                col_stage[0, i : i + 1, lanes] = v[0:1]
                col_stage[1, i : i + 1, lanes] = v[width - 1 : width]
        args = (
            ((xs.at[f], row_halo.at[0]), (hs.at[f], row_halo.at[1])),
            row_send, row_recv, col_stage, col_halo, col_send, col_recv,
        )
        exchange(*args, True)
        exchange(*args, False)

        @pl.when(jnp.logical_and(layer == 0, f + 1 < frame_count))
        def _():
            own_frame(f + 1).start()
            for d in range(1, group):
                frame_copy(f + 1, d).start()

        for k, field in enumerate((xs, hs)):
            def load(i, k=k, field=field):
                if i == 0:
                    return row_halo[k, 0]
                if i == height + 1:
                    return row_halo[k, 1]
                return field[f, i - 1]

            spread(load, col_halo, slice(k * ch, (k + 1) * ch), k * ch)

        pl.when(f == 0)(lambda: copy_wg.wait())
        reset = jax.nn.sigmoid(full(wg, ch) + bias_ref[:, ch : 2 * ch])
        hidden = hs[f].reshape(tile, ch).astype(jnp.float32)
        rs[...] = (reset * hidden).astype(jnp.bfloat16).reshape(height, width, ch)
        for i in range(height):
            v = rs[i].astype(jnp.float32)
            rs_col_stage[0, i : i + 1, :] = v[0:1]
            rs_col_stage[1, i : i + 1, :] = v[width - 1 : width]
        args = (
            ((rs, rs_row_halo),),
            rrow_send, rrow_recv, rs_col_stage, rs_col_halo, rcol_send, rcol_recv,
        )
        exchange(*args, True)
        upd[...] = jax.nn.sigmoid(full(wg, 0) + bias_ref[:, 0:ch])
        pl.when(f == 0)(lambda: copy_wc.wait())
        part[...] = half(wc, 0) + bias_ref[:, 2 * ch : 3 * ch]
        exchange(*args, False)
        pl.when(f > 0)(lambda: send_out(f - 1))

        def load_reset(i):
            if i == 0:
                return rs_row_halo[0]
            if i == height + 1:
                return rs_row_halo[1]
            return rs[i - 1]

        spread(load_reset, rs_col_halo, slice(0, ch), ch)
        candidate = jnp.tanh(part[...] + half(wc, ch))
        update = upd[...]
        hidden = hs[f].reshape(tile, ch).astype(jnp.float32)
        fresh = (1.0 - update) * hidden + update * candidate
        hs[f + 1] = fresh.astype(jnp.bfloat16).reshape(height, width, ch)
        pl.when(layer < last_layer)(lambda: pass_copy(f).start())
        return carry

    def send_out(f):
        own_out(f).start()
        for d in range(1, group):
            out_copy(f, d).start()

    lax.fori_loop(0, frame_count, step, 0)
    send_out(frame_count - 1)

    def finish(f, carry):
        pl.when(layer < last_layer)(lambda: pass_copy(f).wait_send())
        own_out(f).wait()
        for d in range(1, group):
            out_copy(f, d).wait()
        return carry

    lax.fori_loop(0, frame_count, finish, 0)


def shards(count, frames, initial_state, w_gates, w_cand, biases):
    frame_count, strip, cols, ch = frames.shape
    group = 4 if count % 4 == 0 else 1
    height, width = strip * group, cols // group
    dma = pltpu.SemaphoreType.DMA
    bf16, f32 = jnp.bfloat16, jnp.float32
    anywhere = pl.BlockSpec(memory_space=pltpu.HBM)
    rows_k = w_gates.shape[2] * w_gates.shape[3]
    tile = height * width
    return pl.pallas_call(
        functools.partial(kernel, count, group),
        out_shape=jax.ShapeDtypeStruct((1, frame_count, strip, cols, ch), bf16),
        in_specs=[anywhere] * 4 + [pl.BlockSpec(memory_space=pltpu.VMEM)],
        out_specs=anywhere,
        scratch_shapes=[
            pltpu.VMEM((3, rows_k, 2 * ch), bf16),
            pltpu.VMEM((3, rows_k, ch), bf16),
            pltpu.VMEM((frame_count, height, width, ch), bf16),
            pltpu.VMEM((frame_count + 1, height, width, ch), bf16),
            pltpu.VMEM((height, width, ch), bf16),
            pltpu.VMEM(((height + 2) * width, 6 * ch), bf16),
            pltpu.VMEM((tile, ch), f32),
            pltpu.VMEM((tile, ch), f32),
            pltpu.VMEM((2, 2, width, ch), bf16),
            pltpu.VMEM((2, width, ch), bf16),
            pltpu.VMEM((2, height, 2 * ch), f32),
            pltpu.VMEM((6, height, 2 * ch), f32),
            pltpu.VMEM((2, height, ch), f32),
            pltpu.VMEM((6, height, ch), f32),
            dma((2,)), dma((2,)), dma((group,)), dma((group,)),
            dma((frame_count, group)), dma((frame_count, group)),
            dma((frame_count,)), dma((frame_count,)),
            dma((frame_count,)), dma((frame_count, group)), dma((frame_count, group)),
            dma((2, 2)), dma((2, 2)), dma((6,)), dma((6,)),
            dma((1, 2)), dma((1, 2)), dma((6,)), dma((6,)),
        ],
        compiler_params=pltpu.CompilerParams(
            collective_id=0, has_side_effects=True, vmem_limit_bytes=66_000_000
        ),
    )(
        frames,
        initial_state[0],
        w_gates.reshape(3, rows_k, 2 * ch),
        w_cand.reshape(3, rows_k, ch),
        biases,
    )


def solution(mesh):
    placed = (
        P(None, "rows", None, None),
        P("layer", "rows", None, None),
        P("layer", None, None, None, None),
        P("layer", None, None, None, None),
        P("layer", None),
    )
    return jax.shard_map(
        functools.partial(shards, mesh.shape["rows"]),
        mesh=mesh,
        in_specs=placed,
        out_specs=P("layer", None, "rows", None, None),
        check_vma=False,
    )
```

```python
import functools

import jax
import jax.numpy as jnp
from jax import lax
from jax.experimental import pallas as pl
from jax.experimental.pallas import tpu as pltpu
from jax.sharding import PartitionSpec as P

MESH = pltpu.DeviceIdType.MESH if hasattr(pltpu, "DeviceIdType") else pl.DeviceIdType.MESH

COL_DIRS = ((0, -1), (0, 1), (-1, -1), (-1, 1), (1, -1), (1, 1))


def reorder(c, group):
    if group == 4:
        return c + (c // 2) * (5 - 2 * c)
    return c


def kernel(
    count, group, frames_ref, init_ref, wg_ref, wc_ref, bias_ref, out_ref,
    wg, wc, xs, hs, rs, im, upd, part,
    row_halo, rs_row_halo, col_stage, col_halo, rs_col_stage, rs_col_halo,
    w_sem, own_sem, init_send, init_recv, x_send, x_recv, pass_send, pass_recv,
    out_own, out_send, out_recv,
    row_send, row_recv, col_send, col_recv,
    rrow_send, rrow_recv, rcol_send, rcol_recv,
):
    frame_count, strip, cols, ch = frames_ref.shape
    height = strip * group
    width = cols // group
    tile = height * width
    layer = lax.axis_index("layer")
    last_layer = lax.axis_size("layer") - 1
    index = lax.axis_index("rows")
    planes = count // group
    q = index // group
    c = index % group
    t = reorder(c, group)

    def at(plane, tile_index):
        return {"rows": plane * group + reorder(tile_index, group)}

    def guarded(step_row, step_col, action):
        terms = []
        if step_row < 0:
            terms.append(q > 0)
        if step_row > 0:
            terms.append(q < planes - 1)
        if step_col < 0:
            terms.append(t > 0)
        if step_col > 0:
            terms.append(t < group - 1)
        cond = functools.reduce(jnp.logical_and, terms)
        pl.when(cond)(action)

    copy_wg = pltpu.make_async_copy(wg_ref, wg, w_sem.at[0])
    copy_wc = pltpu.make_async_copy(wc_ref, wc, w_sem.at[1])
    own_cols = pl.ds(pl.multiple_of(t * width, width), width)
    own_rows = pl.ds(c * strip, strip)

    def own_init():
        return pltpu.make_async_copy(init_ref.at[:, own_cols, :], hs.at[0, own_rows], own_sem.at[0])

    def own_frame(f):
        return pltpu.make_async_copy(
            frames_ref.at[f, :, own_cols, :], xs.at[f, own_rows], own_sem.at[1]
        )

    def member(d):
        return lax.rem(c + d, group)

    def init_copy(d):
        target = member(d)
        tcols = pl.ds(pl.multiple_of(reorder(target, group) * width, width), width)
        return pltpu.make_async_remote_copy(
            src_ref=init_ref.at[:, tcols, :], dst_ref=hs.at[0, own_rows],
            send_sem=init_send.at[d], recv_sem=init_recv.at[d],
            device_id={"rows": q * group + target}, device_id_type=MESH,
        )

    def frame_copy(f, d):
        target = member(d)
        tcols = pl.ds(pl.multiple_of(reorder(target, group) * width, width), width)
        return pltpu.make_async_remote_copy(
            src_ref=frames_ref.at[f, :, tcols, :], dst_ref=xs.at[f, own_rows],
            send_sem=x_send.at[f, d], recv_sem=x_recv.at[f, d],
            device_id={"rows": q * group + target}, device_id_type=MESH,
        )

    def pass_copy(f):
        return pltpu.make_async_remote_copy(
            src_ref=hs.at[f + 1], dst_ref=xs.at[f],
            send_sem=pass_send.at[f], recv_sem=pass_recv.at[f],
            device_id={"layer": jnp.minimum(layer + 1, last_layer)}, device_id_type=MESH,
        )

    def out_copy(f, d):
        target = member(d)
        return pltpu.make_async_remote_copy(
            src_ref=hs.at[f + 1, pl.ds(target * strip, strip)],
            dst_ref=out_ref.at[0, f, :, own_cols, :],
            send_sem=out_send.at[f, d], recv_sem=out_recv.at[f, d],
            device_id={"rows": q * group + target}, device_id_type=MESH,
        )

    def own_out(f):
        return pltpu.make_async_copy(
            hs.at[f + 1, own_rows], out_ref.at[0, f, :, own_cols, :], out_own.at[f]
        )

    own_init().start()
    pl.when(layer == 0)(lambda: own_frame(0).start())

    row_halo[...] = jnp.zeros_like(row_halo)
    rs_row_halo[...] = jnp.zeros_like(rs_row_halo)
    col_halo[...] = jnp.zeros_like(col_halo)
    rs_col_halo[...] = jnp.zeros_like(rs_col_halo)

    barrier = pltpu.get_barrier_semaphore()

    def greet(where):
        pl.semaphore_signal(barrier, inc=1, device_id=where, device_id_type=MESH)

    for d in range(1, group):
        greet({"rows": q * group + member(d)})
    for step in (-1, 1):
        for side in (-1, 0, 1):
            guarded(step, side, lambda step=step, side=side: greet(at(q + step, t + side)))
    pl.when(layer > 0)(lambda: greet({"layer": layer - 1}))
    pl.when(layer < last_layer)(lambda: greet({"layer": layer + 1}))
    one = lambda cond: jnp.where(cond, 1, 0)
    sideways = 1 + one(t > 0) + one(t < group - 1)
    upright = one(q > 0) + one(q < planes - 1)
    pl.semaphore_wait(
        barrier, group - 1 + sideways * upright + one(layer > 0) + one(layer < last_layer)
    )

    for d in range(1, group):
        init_copy(d).start()

    @pl.when(layer == 0)
    def _():
        for d in range(1, group):
            frame_copy(0, d).start()

    copy_wg.start()
    copy_wc.start()
    own_init().wait()
    for d in range(1, group):
        init_copy(d).wait()

    def exchange(row_pairs, row_out, row_in, stage, halo, col_out, col_in, start):
        def run(copy):
            if start:
                copy.start()
            else:
                copy.wait()

        for side, step in enumerate((-1, 1)):
            for kind, (field, dest) in enumerate(row_pairs):
                def row(side=side, step=step, kind=kind, field=field, dest=dest):
                    run(pltpu.make_async_remote_copy(
                        src_ref=field.at[0 if step < 0 else height - 1],
                        dst_ref=dest.at[1 - side],
                        send_sem=row_out.at[kind, side], recv_sem=row_in.at[kind, 1 - side],
                        device_id=at(q + step, t), device_id_type=MESH,
                    ))

                if start:
                    guarded(step, 0, row)
                else:
                    def both(side=side, step=step, kind=kind, field=field, dest=dest):
                        copy = pltpu.make_async_remote_copy(
                            src_ref=field.at[0], dst_ref=dest.at[side],
                            send_sem=row_out.at[kind, side], recv_sem=row_in.at[kind, side],
                            device_id=at(q + step, t), device_id_type=MESH,
                        )
                        copy.wait()

                    guarded(step, 0, both)
        for k, (dr, dc) in enumerate(COL_DIRS):
            back = COL_DIRS.index((-dr, -dc))

            def col(k=k, back=back, dr=dr, dc=dc):
                copy = pltpu.make_async_remote_copy(
                    src_ref=stage.at[0 if dc < 0 else 1],
                    dst_ref=halo.at[back if start else k],
                    send_sem=col_out.at[k], recv_sem=col_in.at[back if start else k],
                    device_id=at(q + dr, t + dc), device_id_type=MESH,
                )
                run(copy)

            guarded(dr, dc, col)

    first_col = lax.broadcasted_iota(jnp.int32, (width, ch), 0) == 0
    last_col = lax.broadcasted_iota(jnp.int32, (width, ch), 0) == width - 1

    def spread(load, halo, lanes, base):
        for i in range(height + 2):
            v = load(i).astype(jnp.float32)
            if i == 0:
                left = halo[2, height - 1 : height, lanes]
                right = halo[3, height - 1 : height, lanes]
            elif i == height + 1:
                left, right = halo[4, 0:1, lanes], halo[5, 0:1, lanes]
            else:
                left, right = halo[0, i - 1 : i, lanes], halo[1, i - 1 : i, lanes]
            before = jnp.where(first_col, jnp.broadcast_to(left, v.shape), pltpu.roll(v, 1, 0))
            after = jnp.where(
                last_col, jnp.broadcast_to(right, v.shape), pltpu.roll(v, width - 1, 0)
            )
            rows = slice(i * width, (i + 1) * width)
            for b, piece in enumerate((before, v, after)):
                lo = b * 2 * ch + base
                im[rows, lo : lo + ch] = piece.astype(jnp.bfloat16)

    def lhs(a, lo, size):
        return im[a * width : a * width + tile, lo : lo + size]

    def full(weight, n_lo):
        return jnp.dot(
            jnp.concatenate([lhs(a, 0, 6 * ch) for a in range(3)], axis=1),
            weight[:, :, n_lo : n_lo + ch].reshape(18 * ch, ch),
            preferred_element_type=jnp.float32,
        )

    def half(weight, base):
        places = [(a, b * 2 * ch + base) for a in range(3) for b in range(3)]
        return jnp.dot(
            jnp.concatenate([lhs(a, lo, ch) for a, lo in places], axis=1),
            jnp.concatenate([weight[a, lo : lo + ch, :] for a, lo in places], axis=0),
            preferred_element_type=jnp.float32,
        )

    def step(f, carry):
        @pl.when(layer == 0)
        def _():
            own_frame(f).wait()
            for d in range(1, group):
                frame_copy(f, d).wait()

        @pl.when(layer > 0)
        def _():
            pass_copy(f).wait_recv()

        for i in range(height):
            for k, field in enumerate((xs.at[f], hs.at[f])):
                v = field[i].astype(jnp.float32)
                lanes = slice(k * ch, (k + 1) * ch)
                col_stage[0, i : i + 1, lanes] = v[0:1]
                col_stage[1, i : i + 1, lanes] = v[width - 1 : width]
        args = (
            ((xs.at[f], row_halo.at[0]), (hs.at[f], row_halo.at[1])),
            row_send, row_recv, col_stage, col_halo, col_send, col_recv,
        )
        exchange(*args, True)
        exchange(*args, False)

        @pl.when(jnp.logical_and(layer == 0, f + 1 < frame_count))
        def _():
            own_frame(f + 1).start()
            for d in range(1, group):
                frame_copy(f + 1, d).start()

        for k, field in enumerate((xs, hs)):
            def load(i, k=k, field=field):
                if i == 0:
                    return row_halo[k, 0]
                if i == height + 1:
                    return row_halo[k, 1]
                return field[f, i - 1]

            spread(load, col_halo, slice(k * ch, (k + 1) * ch), k * ch)

        pl.when(f == 0)(lambda: copy_wg.wait())
        reset = jax.nn.sigmoid(full(wg, ch) + bias_ref[:, ch : 2 * ch])
        hidden = hs[f].reshape(tile, ch).astype(jnp.float32)
        rs[...] = (reset * hidden).astype(jnp.bfloat16).reshape(height, width, ch)
        for i in range(height):
            v = rs[i].astype(jnp.float32)
            rs_col_stage[0, i : i + 1, :] = v[0:1]
            rs_col_stage[1, i : i + 1, :] = v[width - 1 : width]
        args = (
            ((rs, rs_row_halo),),
            rrow_send, rrow_recv, rs_col_stage, rs_col_halo, rcol_send, rcol_recv,
        )
        exchange(*args, True)
        upd[...] = jax.nn.sigmoid(full(wg, 0) + bias_ref[:, 0:ch])
        pl.when(f == 0)(lambda: copy_wc.wait())
        part[...] = half(wc, 0) + bias_ref[:, 2 * ch : 3 * ch]
        exchange(*args, False)
        pl.when(f > 0)(lambda: send_out(f - 1))

        def load_reset(i):
            if i == 0:
                return rs_row_halo[0]
            if i == height + 1:
                return rs_row_halo[1]
            return rs[i - 1]

        spread(load_reset, rs_col_halo, slice(0, ch), ch)
        candidate = jnp.tanh(part[...] + half(wc, ch))
        update = upd[...]
        hidden = hs[f].reshape(tile, ch).astype(jnp.float32)
        fresh = (1.0 - update) * hidden + update * candidate
        hs[f + 1] = fresh.astype(jnp.bfloat16).reshape(height, width, ch)
        pl.when(layer < last_layer)(lambda: pass_copy(f).start())
        return carry

    def send_out(f):
        own_out(f).start()
        for d in range(1, group):
            out_copy(f, d).start()

    lax.fori_loop(0, frame_count, step, 0)
    send_out(frame_count - 1)

    def finish(f, carry):
        pl.when(layer < last_layer)(lambda: pass_copy(f).wait_send())
        own_out(f).wait()
        for d in range(1, group):
            out_copy(f, d).wait()
        return carry

    lax.fori_loop(0, frame_count, finish, 0)


def shards(count, frames, initial_state, w_gates, w_cand, biases):
    frame_count, strip, cols, ch = frames.shape
    group = 4 if count % 4 == 0 else 1
    height, width = strip * group, cols // group
    dma = pltpu.SemaphoreType.DMA
    bf16, f32 = jnp.bfloat16, jnp.float32
    anywhere = pl.BlockSpec(memory_space=pltpu.HBM)
    rows_k = w_gates.shape[2] * w_gates.shape[3]
    tile = height * width
    return pl.pallas_call(
        functools.partial(kernel, count, group),
        out_shape=jax.ShapeDtypeStruct((1, frame_count, strip, cols, ch), bf16),
        in_specs=[anywhere] * 4 + [pl.BlockSpec(memory_space=pltpu.VMEM)],
        out_specs=anywhere,
        scratch_shapes=[
            pltpu.VMEM((3, rows_k, 2 * ch), bf16),
            pltpu.VMEM((3, rows_k, ch), bf16),
            pltpu.VMEM((frame_count, height, width, ch), bf16),
            pltpu.VMEM((frame_count + 1, height, width, ch), bf16),
            pltpu.VMEM((height, width, ch), bf16),
            pltpu.VMEM(((height + 2) * width, 6 * ch), bf16),
            pltpu.VMEM((tile, ch), f32),
            pltpu.VMEM((tile, ch), f32),
            pltpu.VMEM((2, 2, width, ch), bf16),
            pltpu.VMEM((2, width, ch), bf16),
            pltpu.VMEM((2, height, 2 * ch), f32),
            pltpu.VMEM((6, height, 2 * ch), f32),
            pltpu.VMEM((2, height, ch), f32),
            pltpu.VMEM((6, height, ch), f32),
            dma((2,)), dma((2,)), dma((group,)), dma((group,)),
            dma((frame_count, group)), dma((frame_count, group)),
            dma((frame_count,)), dma((frame_count,)),
            dma((frame_count,)), dma((frame_count, group)), dma((frame_count, group)),
            dma((2, 2)), dma((2, 2)), dma((6,)), dma((6,)),
            dma((1, 2)), dma((1, 2)), dma((6,)), dma((6,)),
        ],
        compiler_params=pltpu.CompilerParams(
            collective_id=0, has_side_effects=True, vmem_limit_bytes=65_500_000
        ),
    )(
        frames,
        initial_state[0],
        w_gates.reshape(3, rows_k, 2 * ch),
        w_cand.reshape(3, rows_k, ch),
        biases,
    )


def solution(mesh):
    placed = (
        P(None, "rows", None, None),
        P("layer", "rows", None, None),
        P("layer", None, None, None, None),
        P("layer", None, None, None, None),
        P("layer", None),
    )
    return jax.shard_map(
        functools.partial(shards, mesh.shape["rows"]),
        mesh=mesh,
        in_specs=placed,
        out_specs=P("layer", None, "rows", None, None),
        check_vma=False,
    )
```
